32 devices in a mesh: band: 4 (over x, core), tr: 4 (over z), tc: 2 (over y).
Axes of the slice: x: 2, y: 2, z: 4, core: 2. Of those that a mesh axis runs over, the one named last changes fastest.
Arguments:
- voltages: bfloat16 [4096, 2, 1024], P(('band', 'tr', 'tc')), parts along dimension 0, may hold values from -4 to 4
Outputs:
- visibilities: bfloat16 [128, 2, 1024, 1024], P(('band', 'tc'), None, 'tr'), parts along dimension 0
The draws below stay inside these ranges and needn't reach their ends.
There are 4 independent parts, one for each index of `band`. The reference program is written for one: setup_inputs(seed, part) draws one part's arguments, and reference() takes and returns one part's arrays. A program takes and returns all parts, laid end to end along the dimension named above; each array names one. Nothing has to cross between parts.
All inputs are finite; a program needn't handle non-finite values.
Results may differ from the reference program's by a relative error of at most 0.0054.
Values may be sent and summed in bfloat16 or wider, within the bound.
No kernel may reach another device: no remote copies, remote signals or barrier semaphores. Data moves between devices by JAX's collectives and lax.ppermute only.
A program may use at most 64 MiB of HBM per device.

```python
import math
import jax
import jax.numpy as jnp
from jax import lax

INPUTS = 1024
FINE = 32
TAPS = 16
SPECTRA = 32
SAMPLES = 1024


def level_of(rng, dims, shards, smallest, largest):
    def one(dim, shards_of):
        draws = jax.random.uniform(jax.random.fold_in(jax.random.fold_in(rng, 6), dim), (shards_of,), jnp.float32, smallest / len(shards), largest / len(shards))
        return jnp.repeat(jnp.exp(draws), dims[dim] // shards_of).reshape((-1,) + (1,) * (len(dims) - dim - 1))

    level = one(*shards[0])
    for cut in shards[1:]:
        level = level * one(*cut)
    return level


def noise(rng, extent, spread, bound, pieces=(), kind=jnp.bfloat16):
    gain = level_of(rng, extent, pieces, -0.22, 0.18) if pieces else 1.0
    array = jax.random.normal(rng, extent, jnp.float32) * spread * gain
    return jnp.minimum(jnp.maximum(array, -bound), bound).astype(kind)


def setup_inputs(seed: int = 0, part: int = 0) -> dict:
    splits = jax.random.split(jax.random.key(seed), 2)
    part_splits = jax.random.split(jax.random.fold_in(splits[1], part), 2)
    return {
        "voltages": noise(part_splits[0], (SAMPLES, 2, INPUTS), 1.0, 4.0, ((0, 8),)),
    }


def filter_taps(tap_total, fine_total):
    length = tap_total * fine_total
    position = jnp.arange(length).astype(jnp.float32)
    offset = (position - (length - 1) / 2.0) / fine_total
    prototype = jnp.sin(math.pi * offset) / (math.pi * offset)
    prototype = prototype / jnp.sqrt(jnp.sum(prototype * prototype))
    return prototype.reshape(tap_total, fine_total)

def fourier_table(fine_total):
    indices = jnp.arange(fine_total).astype(jnp.float32)
    angles = 2.0 * math.pi * jnp.mod(indices[:, None] * indices[None, :], fine_total) / fine_total
    cosine = jnp.cos(angles)
    sine_part = jnp.sin(angles)
    stacked = jnp.stack([jnp.stack([cosine, -sine_part], axis=-1), jnp.stack([sine_part, cosine], axis=-1)], axis=1)
    return stacked.reshape(2 * fine_total, 2 * fine_total)

def reference(voltages):
    tap_table = filter_taps(TAPS, FINE)
    fourier = fourier_table(FINE)
    leading = jnp.zeros(((TAPS - 1) * FINE, 2, INPUTS), voltages.dtype)
    padded = jnp.concatenate([leading, voltages], axis=0).reshape(SPECTRA + TAPS - 1, FINE, 2, INPUTS)
    weighted = jnp.zeros((SPECTRA, FINE, 2, INPUTS), jnp.float32)
    for tap_index in range(TAPS):
        weighted = weighted + tap_table[tap_index][None, :, None, None] * padded[tap_index:tap_index + SPECTRA].astype(jnp.float32)
    spectra = jnp.einsum('sjm,jo->som', weighted.reshape(SPECTRA, 2 * FINE, INPUTS), fourier, precision=lax.Precision.HIGHEST)
    spectra = spectra.reshape(SPECTRA, FINE, 2, INPUTS).astype(jnp.bfloat16)
    channel_major = jnp.transpose(spectra, (1, 0, 2, 3)).astype(jnp.float32)

    def one_channel(channel_block):
        swapped = jnp.stack([channel_block[:, 1], -channel_block[:, 0]], axis=1)
        stacked = jnp.stack([channel_block, swapped], axis=0)
        return jnp.einsum('rsci,scj->rij', stacked, channel_block, precision=lax.Precision.HIGHEST)
    summed = lax.map(one_channel, channel_major)
    return (summed / float(SPECTRA)).astype(jnp.bfloat16)
```

```python
import math

import jax
import jax.numpy as jnp
import numpy as np
from jax import lax
from jax.experimental import pallas as pl
from jax.experimental.pallas import tpu as pltpu
from jax.sharding import PartitionSpec as P

FINE = 32
TAPS = 16


def shifted(block, axis, distance):
    devices = range(lax.axis_size(axis))
    route = [(i - distance, i) for i in devices if i - distance in devices]
    return lax.ppermute(block, axis, route)


def filter_taps(tap_total, fine_total):
    length = tap_total * fine_total
    position = jnp.arange(length).astype(jnp.float32)
    offset = (position - (length - 1) / 2.0) / fine_total
    prototype = jnp.sin(math.pi * offset) / (math.pi * offset)
    prototype = prototype / jnp.sqrt(jnp.sum(prototype * prototype))
    return prototype.reshape(tap_total, fine_total)


def fourier_table(fine_total):
    indices = jnp.arange(fine_total).astype(jnp.float32)
    angles = 2.0 * math.pi * jnp.mod(indices[:, None] * indices[None, :], fine_total) / fine_total
    cosine = jnp.cos(angles)
    sine_part = jnp.sin(angles)
    stacked = jnp.stack(
        [jnp.stack([cosine, -sine_part], axis=-1), jnp.stack([sine_part, cosine], axis=-1)], axis=1
    )
    return stacked.reshape(2 * fine_total, 2 * fine_total)


def filterbank(extended, hop_count):
    inputs = extended.shape[3]
    tap_table = filter_taps(TAPS, FINE)
    fourier = fourier_table(FINE)
    weighted = jnp.zeros((hop_count, FINE, 2, inputs), jnp.float32)
    for tap_index in range(TAPS):
        weighted = weighted + tap_table[tap_index][None, :, None, None] * extended[
            tap_index : tap_index + hop_count
        ].astype(jnp.float32)
    spectra = jnp.einsum(
        "sjm,jo->som",
        weighted.reshape(hop_count, 2 * FINE, inputs),
        fourier,
        precision=lax.Precision.HIGHEST,
    )
    return spectra.reshape(hop_count, FINE, 2, inputs).astype(jnp.bfloat16)


def streamed(voltages):
    samples = voltages.shape[0]
    inputs = voltages.shape[2]
    hop_count = samples // FINE
    needed = TAPS - 1
    shift_count = (needed + hop_count - 1) // hop_count
    earlier = []
    for distance in range(1, shift_count + 1):
        take_hops = min(hop_count, needed - (distance - 1) * hop_count)
        portion = voltages[samples - take_hops * FINE :]
        arrived = shifted(portion, ("tr", "tc"), distance)
        earlier = [arrived] + earlier
    extended = jnp.concatenate(earlier + [voltages], axis=0).reshape(
        needed + hop_count, FINE, 2, inputs
    )
    spectra = filterbank(extended, hop_count)
    turned = lax.all_to_all(
        lax.all_to_all(spectra, "tr", split_axis=3, concat_axis=0, tiled=True),
        "tc",
        split_axis=1,
        concat_axis=0,
        tiled=True,
    )
    spectra_total = turned.shape[0]
    swapped = jnp.stack([turned[:, :, 1], -turned[:, :, 0]], axis=2)
    stacked = jnp.stack([turned, swapped], axis=0)
    inverse_total = 1.0 / float(spectra_total)
    product = jnp.einsum(
        "rskci,skcj->krij",
        stacked,
        lax.all_gather(turned, "tr", axis=3, tiled=True),
        preferred_element_type=jnp.float32,
    )
    summed = product * inverse_total
    return summed.astype(jnp.bfloat16)


def stacked_operator(hops):
    position = np.arange(TAPS * FINE, dtype=np.float64)
    offset = (position - (TAPS * FINE - 1) / 2.0) / FINE
    prototype = np.sinc(offset)
    taps = (prototype / np.sqrt(np.sum(prototype * prototype))).reshape(TAPS, FINE)
    indices = np.arange(FINE)
    angles = 2.0 * np.pi * np.mod(np.outer(indices, indices), FINE) / FINE
    cosine, sine = np.cos(angles), np.sin(angles)
    fourier = np.stack([np.stack([cosine, -sine], -1), np.stack([sine, cosine], -1)], 1)
    reach = (TAPS - 2 + hops) // hops + 1
    matrix = np.zeros((reach, FINE, 2, hops, hops, FINE, 2))
    for distance in range(reach):
        for out_hop in range(hops):
            for in_hop in range(hops):
                tap = in_hop - out_hop + TAPS - 1 - hops * distance
                if 0 <= tap < TAPS:
                    weighted = taps[tap][:, None, None, None] * fourier
                    matrix[distance, :, :, out_hop, in_hop] = weighted.transpose(2, 3, 0, 1)
    return matrix.reshape(reach, FINE, 2 * hops, hops * FINE * 2)


def split_in_two(matrix):
    high = matrix.astype(np.float32).astype(jnp.bfloat16)
    low = (matrix - high.astype(np.float64)).astype(np.float32).astype(jnp.bfloat16)
    return high, low


def correlate(blocks, places, valid, operator, row_block, blocks_total, rows_total):
    wide, inputs = blocks[0].shape
    reach_rows = operator.shape[1]
    channels = operator.shape[3]
    count = len(blocks)
    per_block = operator.shape[4]
    step_rows = channels * per_block
    half = per_block // 2
    spectra_total = blocks_total * half
    scale = 1.0 / float(spectra_total)

    def kernel(info, operator_ref, *refs):
        block_refs, out_ref, sums = refs[:count], refs[count], refs[count + 1]
        channel = pl.program_id(0)

        @pl.when(channel == 0)
        def _():
            sums[...] = jnp.zeros_like(sums)
            high = operator_ref[0].reshape(reach_rows * step_rows, wide)
            low = operator_ref[1].reshape(reach_rows * step_rows, wide)
            for b in range(count):

                @pl.when(info[count + b] == 1)
                def _(b=b):
                    block = block_refs[b][...]
                    start = pl.multiple_of(info[b] * step_rows, step_rows)
                    where = pl.ds(start, reach_rows * step_rows)
                    sums[where, :] += jnp.dot(
                        high, block, preferred_element_type=jnp.float32
                    ) + jnp.dot(low, block, preferred_element_type=jnp.float32)

        first = pl.multiple_of(info[2 * count] * rows_total, rows_total)
        everything, rows, turned = [], [], []
        sign = jnp.where(
            lax.broadcasted_iota(jnp.int32, (per_block, rows_total), 0) < half, 1.0, -1.0
        )
        for s in range(blocks_total):
            place = pl.multiple_of(s * step_rows + channel * per_block, per_block)
            everything.append(sums[pl.ds(place, per_block), :])
            mine = sums[pl.ds(place, per_block), pl.ds(first, rows_total)]
            rows.append(mine)
            turned.append(pltpu.roll(mine, half, 0) * sign)
        right = jnp.concatenate(everything, 0).astype(jnp.bfloat16)
        for part, pieces in enumerate((rows, turned)):
            left = jnp.concatenate(pieces, 0).astype(jnp.bfloat16)
            product = lax.dot_general(
                left, right, (((0,), (0,)), ((), ())), preferred_element_type=jnp.float32
            )
            out_ref[0, part] = (product * scale).astype(jnp.bfloat16)

    info = jnp.stack(
        [jnp.asarray(v, jnp.int32) for v in (*places, *valid, row_block[0], row_block[1])]
    )
    at = 2 * count + 1
    return pl.pallas_call(
        kernel,
        grid_spec=pltpu.PrefetchScalarGridSpec(
            num_scalar_prefetch=1,
            grid=(channels,),
            in_specs=[
                pl.BlockSpec(
                    (2, reach_rows, None, channels, per_block, wide),
                    lambda k, info: (0, 0, info[at], 0, 0, 0),
                )
            ]
            + [pl.BlockSpec((wide, inputs), lambda k, info: (0, 0))] * count,
            out_specs=pl.BlockSpec((1, 2, rows_total, inputs), lambda k, info: (k, 0, 0, 0)),
            scratch_shapes=[
                pltpu.VMEM(((blocks_total + reach_rows - 1) * step_rows, inputs), jnp.float32)
            ],
        ),
        out_shape=jax.ShapeDtypeStruct((channels, 2, rows_total, inputs), jnp.bfloat16),
        compiler_params=pltpu.CompilerParams(vmem_limit_bytes=48 * 2**20),
        name="filter_and_correlate",
    )(info, operator, *blocks)


def gathered(voltages):
    samples, _, inputs = voltages.shape
    hops = samples // FINE
    line, pair = lax.axis_size("tr"), lax.axis_size("tc")
    here, side = lax.axis_index("tr"), lax.axis_index("tc")
    own = voltages.reshape(samples * 2, inputs)

    def across(block):
        return lax.ppermute(block, "tc", [(0, 1), (1, 0)])

    far = lax.ppermute(own, "tr", [(i, i ^ 2) for i in range(line)])
    up = lax.ppermute(own, "tr", [(0, 1), (1, 2), (2, 3)])
    down = lax.ppermute(own, "tr", [(1, 0), (2, 1), (3, 2)])
    end = lax.ppermute(far, "tr", [(2, 3), (1, 0)])
    lines = [
        (own, here, 1),
        (up, here - 1, here > 0),
        (down, here + 1, here < line - 1),
        (far, here ^ 2, 1),
        (end, line - 1 - here, (here == 0) | (here == line - 1)),
    ]
    blocks, places, valid = [], [], []
    for block, place, ok in lines:
        for array, which in ((block, side), (across(block), 1 - side)):
            blocks.append(array)
            places.append(jnp.clip(place, 0, line - 1) * pair + which)
            valid.append(ok)
    matrix = stacked_operator(hops)
    reach = matrix.shape[0]
    matrix = matrix.reshape(reach, pair, FINE // pair, 2 * hops, samples * 2)
    operator = jnp.asarray(np.stack(split_in_two(matrix)))
    return correlate(
        blocks, places, valid, operator, (here, side), line * pair, inputs // line
    )


def solution(mesh):
    in_specs = (P(("band", "tr", "tc"), None, None),)
    out_specs = P(("band", "tc"), None, "tr", None)
    small = mesh.shape["tr"] == 4 and mesh.shape["tc"] == 2
    return jax.shard_map(
        gathered if small else streamed,
        mesh=mesh,
        in_specs=in_specs,
        out_specs=out_specs,
        check_vma=False,
    )
```
